32 devices in a mesh: row: 4 (over y, x), col: 8 (over z, core).
Axes of the slice: x: 2, y: 2, z: 4, core: 2. Of those that a mesh axis runs over, the one named last changes fastest.
Arguments:
- tiles: float32 [384, 1024, 128], P('row', 'col'), may hold values from -0.1875 to 0.1875
- tile_row: int32 [384, 8], P('row', 'col'), may hold values from 0 to 511
- tile_col: int32 [384, 8], P('row', 'col'), may hold values from 0 to 255
- tile_count: int32 [4, 8], P('row', 'col'), may hold values from 24 to 96, as said below
- cost: float32 [8, 32768], P('col', 'row'), may hold values from -6 to 6
- rhs: float32 [4, 65536], P('row', 'col'), may hold values from -6 to 6
- lower: float32 [8, 32768], P('col', 'row'), may hold values from -2 to -0.3
- upper: float32 [8, 32768], P('col', 'row'), may hold values from 0.3 to 2
- primal_start: float32 [8, 32768], P('col', 'row'), may hold values from -0.3 to 0.3
- dual_start: float32 [4, 65536], P('row', 'col'), may hold values from 0 to 1
Outputs:
- primal_mean: float32 [8, 32768], P('col', 'row')
- dual_mean: float32 [4, 65536], P('row', 'col')
- primal_last: float32 [8, 32768], P('col', 'row')
- dual_last: float32 [4, 65536], P('row', 'col')
The draws below stay inside these ranges and needn't reach their ends.
Inputs may be any that keep to these rules, and one draw needn't show every extreme that they name: `tile_count`: live tiles of each device; some device holds 96.
All inputs are finite; a program needn't handle non-finite values.
Results may differ from the reference program's by a relative error of at most 0.0001.
Values sent between devices are 32-bit elements; how exact they have to be, the bound alone decides.
A program may use at most 64 MiB of HBM per device.

```python
import jax
import jax.numpy as jnp
from jax import lax

BS = 128
M = 262144
N = 262144
TILES = 96
ITERS = 6
N_ROW = 4
N_COL = 8


def draw_tile_count(key, part):
    devices_all = N_ROW * N_COL
    counts = jax.random.randint(key, (devices_all,), TILES // 4, TILES + 1)
    chosen = jax.random.randint(jax.random.fold_in(key, 7), (), 0, devices_all)
    counts = jnp.where(jnp.arange(devices_all) == chosen, TILES, counts)
    return counts.reshape(N_ROW, N_COL).astype(jnp.int32)


def plant(array, own_key, smallest, top_value):
    place = [jax.random.randint(jax.random.fold_in(own_key, axis), (), 0, length) for axis, length in enumerate(array.shape)]
    main_axis = array.shape.index(max(array.shape))
    next_to = place[:main_axis] + [(place[main_axis] + 1) % array.shape[main_axis]] + place[main_axis + 1:]
    return array.at[tuple(place)].set(smallest).at[tuple(next_to)].set(top_value)


def level_of(own_key, extent, cuts, least, largest):
    level, own = 1.0, jax.random.fold_in(own_key, 6)
    for position, shards_of in cuts:
        draws = jnp.exp(jax.random.uniform(jax.random.fold_in(own, position), (shards_of,), jnp.float32, least / len(cuts), largest / len(cuts)))
        level = level * jnp.repeat(draws, extent[position] // shards_of).reshape([-1 if axis == position else 1 for axis in range(len(extent))])
    return level


def bell_draw(rng, extent, scale, limit, cuts=(), kind=jnp.bfloat16):
    level = level_of(rng, extent, cuts, -0.22, 0.18) if cuts else 1.0
    array = jax.random.normal(rng, extent, jnp.float32) * scale * level
    return jnp.minimum(jnp.maximum(array, -limit), limit).astype(kind)


def setup_inputs(seed: int = 0) -> dict:
    arg_keys = jax.random.split(jax.random.key(seed), 11)
    return {
        "tiles": bell_draw(arg_keys[0], (N_ROW * TILES, N_COL * BS, BS), (BS * N_COL) ** -0.5, 0.1875, ((0, 4), (1, 8)), jnp.float32),
        "tile_row": plant(jax.random.randint(arg_keys[1], (N_ROW * TILES, N_COL), 0, M // (BS * N_ROW)), jax.random.fold_in(arg_keys[1], 1), 0, (M // (BS * N_ROW)) - 1).astype(jnp.int32),
        "tile_col": plant(jax.random.randint(arg_keys[2], (N_ROW * TILES, N_COL), 0, N // (BS * N_COL)), jax.random.fold_in(arg_keys[2], 1), 0, (N // (BS * N_COL)) - 1).astype(jnp.int32),
        "tile_count": draw_tile_count(jax.random.fold_in(arg_keys[10], 71), 0),
        "cost": bell_draw(arg_keys[4], (N_COL, N // N_COL), 1.0, 6.0, ((0, 8), (1, 4)), jnp.float32),
        "rhs": bell_draw(arg_keys[5], (N_ROW, M // N_ROW), 1.0, 6.0, ((0, 4), (1, 8)), jnp.float32),
        "lower": jnp.clip(-2.0 + 1.7 * jax.random.uniform(arg_keys[6], (N_COL, N // N_COL), jnp.float32) ** level_of(arg_keys[6], (N_COL, N // N_COL), ((0, 8), (1, 4)), -0.2, 0.2), -2.0, -0.3),
        "upper": jnp.clip(0.3 + 1.7 * jax.random.uniform(arg_keys[7], (N_COL, N // N_COL), jnp.float32) ** level_of(arg_keys[7], (N_COL, N // N_COL), ((0, 8), (1, 4)), -0.2, 0.2), 0.3, 2.0),
        "primal_start": jnp.clip(jax.random.uniform(arg_keys[8], (N_COL, N // N_COL), jnp.float32, -0.3, 0.3) * level_of(arg_keys[8], (N_COL, N // N_COL), ((0, 8), (1, 4)), -0.4, 0.0), -0.3, 0.3),
        "dual_start": jnp.clip(1.0 * jax.random.uniform(arg_keys[9], (N_ROW, M // N_ROW), jnp.float32) ** level_of(arg_keys[9], (N_ROW, M // N_ROW), ((0, 4), (1, 8)), -0.2, 0.2), 0.0, 1.0),
    }


exact = lax.Precision.HIGHEST
primal_step = 0.3
dual_step = 0.3


def reference(tiles, tile_row, tile_col, tile_count, cost, rhs, lower, upper, primal_start, dual_start):
    row_blocks = M // (BS * N_ROW)
    col_blocks = N // (BS * N_COL)
    blocks = tiles.reshape(N_ROW, TILES, N_COL, BS, BS)
    rows_index = tile_row.reshape(N_ROW, TILES, N_COL)
    cols_index = tile_col.reshape(N_ROW, TILES, N_COL)
    live = (jnp.arange(TILES, dtype=jnp.int32)[None, :, None] < tile_count[:, None, :]).astype(jnp.float32)
    row_hot = (rows_index[..., None] == jnp.arange(row_blocks, dtype=jnp.int32)).astype(jnp.float32) * live[..., None]
    col_hot = (cols_index[..., None] == jnp.arange(col_blocks, dtype=jnp.int32)).astype(jnp.float32)

    def forward(primal_blocks):
        def single(pieces):
            block_part, hot_rows, hot_cols = pieces
            taken = jnp.einsum('tck,ckj->tcj', hot_cols, primal_blocks, precision=exact)
            product = jnp.einsum('tcij,tcj->tci', block_part, taken, precision=exact)
            return jnp.einsum('tcr,tci->ri', hot_rows, product, precision=exact)
        return lax.map(single, (blocks, row_hot, col_hot))

    def backward(dual_blocks):
        def single(pieces):
            block_part, hot_rows, hot_cols, dual_part = pieces
            taken = jnp.einsum('tcr,ri->tci', hot_rows, dual_part, precision=exact)
            product = jnp.einsum('tcij,tci->tcj', block_part, taken, precision=exact)
            return jnp.einsum('tck,tcj->ckj', hot_cols, product, precision=exact)
        return jnp.sum(lax.map(single, (blocks, row_hot, col_hot, dual_blocks)), axis=0)

    primal = primal_start.reshape(N_COL, col_blocks, BS)
    dual = dual_start.reshape(N_ROW, row_blocks, BS)
    cost_blocks = cost.reshape(N_COL, col_blocks, BS)
    lower_blocks = lower.reshape(N_COL, col_blocks, BS)
    upper_blocks = upper.reshape(N_COL, col_blocks, BS)
    rhs_blocks = rhs.reshape(N_ROW, row_blocks, BS)
    extrapolated = primal
    primal_total = jnp.zeros_like(primal)
    dual_total = jnp.zeros_like(dual)
    for iteration in range(ITERS):
        dual = jnp.maximum(dual + dual_step * (rhs_blocks - forward(extrapolated)), 0.0)
        moved = primal - primal_step * (cost_blocks - backward(dual))
        primal_new = jnp.minimum(jnp.maximum(moved, lower_blocks), upper_blocks)
        extrapolated = 2.0 * primal_new - primal
        primal = primal_new
        primal_total = primal_total + primal
        dual_total = dual_total + dual
    shape_primal = (N_COL, N // N_COL)
    shape_dual = (N_ROW, M // N_ROW)
    return ((primal_total / ITERS).reshape(shape_primal), (dual_total / ITERS).reshape(shape_dual),
            primal.reshape(shape_primal), dual.reshape(shape_dual))
```

```python
import functools

import jax
import jax.numpy as jnp
from jax import lax
from jax.experimental import pallas as pl
from jax.experimental.pallas import tpu as pltpu
from jax.sharding import PartitionSpec as P

ITERS = 6
primal_step = 0.3
dual_step = 0.3
SUB = 8
CHUNKS = 3
TILE_PARTS = 4
UNROLL = 4
VMEM_BYTES = 48 * 1024 * 1024


def split_dot(hot, data):
    high = data.astype(jnp.bfloat16)
    rest = data - high.astype(jnp.float32)
    middle = rest.astype(jnp.bfloat16)
    low = (rest - middle.astype(jnp.float32)).astype(jnp.bfloat16)
    dot = functools.partial(jnp.dot, preferred_element_type=jnp.float32)
    return (dot(hot, low) + dot(hot, middle)) + dot(hot, high)


def pieces_of(data):
    high = data.astype(jnp.bfloat16).astype(jnp.float32)
    rest = data - high
    middle = rest.astype(jnp.bfloat16).astype(jnp.float32)
    return high, middle, rest - middle


def kernel(
    n_row, n_col,
    tiles_hbm, tile_row, tile_col, tile_count, cost, rhs, lower, upper, primal_start, dual_start,
    primal_mean, dual_mean, primal_last, dual_last,
    tiles, plain, flipped, y_init, x_init, b_init, c_init, z_all, p_all, y_hot, x_hot, y_column, x_column,
    y_state, b_state, x_state, c_state, l_state, u_state, extrapolated, y_total, x_total,
    row_line, col_line, count_cell, tile_sem, in_sem, z_send, z_recv, p_send, p_recv,
    yi_send, yi_recv, bi_send, bi_recv, xi_send, xi_recv, ci_send, ci_recv,
):
    slots = tile_row.shape[1]
    size = slots // CHUNKS
    sy = rhs.shape[0]
    sx = cost.shape[0]
    row = lax.axis_index("row")
    col = lax.axis_index("col")
    chips = n_col // 2
    chip = col // 2
    core = col % 2
    partner = chip * 2 + (1 - core)
    high_half = (chip * 2) // chips

    def chip_at(k):
        down = chips - 1 - k
        down = down - (chip - down + chips) // chips
        up = k + (k - chip + chips) // chips
        return (1 - high_half) * down + high_half * up

    def row_to(d):
        return (row + d) % n_row

    def row_from(d):
        return (row + n_row - d) % n_row

    local = [
        pltpu.make_async_copy(source, place, in_sem.at[i])
        for i, (source, place) in enumerate(
            [
                (primal_start, x_init.at[row, 0:sx]),
                (dual_start, y_init.at[col, 0:sy]),
                (rhs, b_init.at[col]),
                (cost, c_init.at[row, 0:sx]),
                (lower, c_init.at[row, sx : 2 * sx]),
                (upper, c_init.at[row, 2 * sx : 3 * sx]),
                (tile_row, row_line),
                (tile_col, col_line),
                (tile_count, count_cell),
            ]
        )
    ]
    for copy in local:
        copy.start()
    part = slots // TILE_PARTS
    tile_copies = [
        pltpu.make_async_copy(
            tiles_hbm.at[i * part : (i + 1) * part], tiles.at[i * part : (i + 1) * part], tile_sem.at[i]
        )
        for i in range(TILE_PARTS)
    ]
    for copy in tile_copies:
        copy.start()

    mesh_id = pl.DeviceIdType.MESH
    barrier = pltpu.get_barrier_semaphore()
    for d in range(1, n_row):
        pl.semaphore_signal(barrier, inc=1, device_id={"row": row_to(d)}, device_id_type=mesh_id)
    for k in range(chips - 1):
        pl.semaphore_signal(
            barrier, inc=1, device_id={"col": chip_at(k) * 2 + core}, device_id_type=mesh_id
        )
    pl.semaphore_signal(barrier, inc=1, device_id={"col": partner}, device_id_type=mesh_id)

    for copy in local[6:]:
        copy.wait()
    live = lax.broadcasted_iota(jnp.int32, (1, slots), 1) < count_cell[...]
    for ids, init, me, at in ((row_line, y_init, col, sy), (col_line, x_init, row, sx)):
        init[me, at : at + SUB, :] = jnp.full((SUB, 128), -1.0, jnp.float32)
        init[me, at : at + SUB, 0:slots] = jnp.broadcast_to(
            jnp.where(live, ids[...].astype(jnp.float32), -1.0), (SUB, slots)
        )

    def remote(place, send, recv, target):
        return pltpu.make_async_remote_copy(
            src_ref=place, dst_ref=place, send_sem=send, recv_sem=recv, device_id=target, device_id_type=mesh_id
        )

    def row_send(place_of, send, recv, c):
        for d in range(1, n_row):
            remote(place_of(row, c), send(d - 1, c), recv(d - 1, c), {"row": row_to(d)}).start()

    def row_arrive(place_of, send, recv, c):
        for d in range(1, n_row):
            remote(place_of(row_from(d), c), send(d - 1, c), recv(d - 1, c), {"row": row_to(d)}).wait_recv()

    def row_sent(place_of, send, recv, c):
        for d in range(1, n_row):
            remote(place_of(row, c), send(d - 1, c), recv(d - 1, c), {"row": row_to(d)}).wait_send()

    to_partner = {"col": partner}

    def col_send(place_of, send, recv, c):
        for k in range(chips - 1):
            there = chip_at(k)
            remote(place_of(col, c), send(there, c), recv(chip, c), {"col": there * 2 + core}).start()
        remote(place_of(col, c), send(chip, c), recv(chip, c), to_partner).start()

    def col_arrive(place_of, send, recv, c):
        for k in reversed(range(chips - 1)):
            there = chip_at(k)
            block = place_of(there * 2 + core, c)
            remote(block, send(there, c), recv(there, c), to_partner).wait_recv()
            remote(block, send(chips + there, c), recv(chips + there, c), to_partner).start()

    def col_complete(place_of, send, recv, c):
        remote(place_of(partner, c), send(chip, c), recv(chip, c), to_partner).wait_recv()
        for k in reversed(range(chips - 1)):
            there = chip_at(k)
            block = place_of(there * 2 + 1 - core, c)
            remote(block, send(chips + there, c), recv(chips + there, c), to_partner).wait_recv()

    def col_sent(place_of, send, recv, c):
        for k in reversed(range(chips - 1)):
            there = chip_at(k)
            remote(place_of(col, c), send(there, c), recv(chip, c), to_partner).wait_send()
            block = place_of(there * 2 + core, c)
            remote(block, send(chips + there, c), recv(chips + there, c), to_partner).wait_send()
        remote(place_of(col, c), send(chip, c), recv(chip, c), to_partner).wait_send()

    def whole(buffer, send, recv):
        return (lambda i, c: buffer.at[i], lambda k, c: send.at[k], lambda k, c: recv.at[k])

    def sliced(buffer, send, recv, now):
        return (
            lambda i, c: buffer.at[now, c, i],
            lambda k, c: send.at[now, k, c],
            lambda k, c: recv.at[now, k, c],
        )

    xi = whole(x_init, xi_send, xi_recv)
    ci = whole(c_init, ci_send, ci_recv)
    yi = whole(y_init, yi_send, yi_recv)
    bi = whole(b_init, bi_send, bi_recv)
    local[0].wait()
    pl.semaphore_wait(barrier, (n_row - 1) + (chips - 1) + 1)
    row_send(*xi, 0)
    for copy in local[1:3]:
        copy.wait()
    y_init[col, 0:sy, :] = y_init[col, 0:sy, :] + dual_step * b_init[col]
    col_send(*yi, 0)

    def pair_up(q, carry):
        for half in range(2):
            tile = tiles[2 * q + half]
            for out, data in ((plain, tile), (flipped, tile.T)):
                high = data.astype(jnp.bfloat16)
                out[q, 0:128, half * 128 : half * 128 + 128] = high
                out[q, 128:256, half * 128 : half * 128 + 128] = (
                    data - high.astype(jnp.float32)
                ).astype(jnp.bfloat16)
        return carry

    for i in range(TILE_PARTS):
        tile_copies[i].wait()
        lax.fori_loop(i * part // 2, (i + 1) * part // 2, pair_up, 0, unroll=2)

    def column_of(init, i, at):
        return init[i, at : at + SUB, :].T[:slots, 0:1]

    def own_ids(init, me, at):
        ids = column_of(init, me, at)
        return jnp.where(ids < 0.0, -2.0, ids)

    def hot_of(ids, first, share, column, hot, init, at, n):
        for i in range(n):
            ids_of = jnp.broadcast_to(column_of(init, i, at), (slots, 128))
            for c in range(CHUNKS):
                start = (c * n + i) * size
                column[start : start + size, :] = ids_of[c * size : (c + 1) * size, :]
        wide_all = column[...].T[0:1, :]
        own = (first + lax.broadcasted_iota(jnp.int32, (share, 1), 0)).astype(jnp.float32)
        for c in range(CHUNKS):
            wide = wide_all[:, c * n * size : (c + 1) * n * size]
            hot[c, 0:slots, :] = jnp.where(ids == wide, 1.0, 0.0).astype(jnp.bfloat16)
            hot[c, slots : slots + share, :] = jnp.where(own == wide, 1.0, 0.0).astype(jnp.bfloat16)

    def pick_of(ids, blocks):
        lanes = lax.broadcasted_iota(jnp.int32, (slots, blocks), 1).astype(jnp.float32)
        return jnp.where(ids == lanes, 1.0, 0.0).astype(jnp.bfloat16)

    def place_state(state, pick, init, at, share, me, n):
        state[0:slots, :] = split_dot(pick, init[:, at : at + share, :].reshape(n * share, 128))
        state[slots : slots + share, :] = init[me, at : at + share, :]

    def products(pairs, vectors, out, send):
        line = lax.broadcasted_iota(jnp.int32, (SUB, 128), 0)
        per_chunk = slots // SUB // CHUNKS

        for c in range(CHUNKS):
            place = out(c)

            def group(i, carry):
                g = c * per_chunk + i
                at = pl.multiple_of(g * SUB, SUB)
                left = jnp.concatenate(pieces_of(vectors[pl.ds(at, SUB), :]), axis=0).astype(jnp.bfloat16)
                left = jnp.concatenate([left, left], axis=1)
                result = jnp.zeros((SUB, 128), jnp.float32)
                for q in range(SUB // 2):
                    both = jnp.dot(left, pairs[g * (SUB // 2) + q], preferred_element_type=jnp.float32)
                    total = (both[2 * SUB :] + both[SUB : 2 * SUB]) + both[:SUB]
                    result = jnp.where(line == 2 * q, total[:, :128], result)
                    result = jnp.where(line == 2 * q + 1, total[:, 128:], result)
                place[pl.ds(pl.multiple_of(i * SUB, SUB), SUB), :] = result
                return carry

            lax.fori_loop(0, per_chunk, group, 0, unroll=UNROLL)
            send(c)

    def forward(now):
        z = sliced(z_all, z_send, z_recv, now)
        products(
            flipped, extrapolated, lambda c: z_all.at[now, c, col], lambda c: col_send(*z, c)
        )

    row_arrive(*xi, 0)
    col_ids = own_ids(x_init, row, sx)
    x_pick = pick_of(col_ids, n_row * sx)
    place_state(x_state, x_pick, x_init, 0, sx, row, n_row)
    extrapolated[...] = x_state[0:slots, :]
    forward(0)
    for copy in local[3:6]:
        copy.wait()
    row_send(*ci, 0)
    hot_of(col_ids, row * sx, sx, x_column, x_hot, x_init, sx, n_row)
    col_arrive(*yi, 0)
    col_complete(*yi, 0)
    row_ids = own_ids(y_init, col, sy)
    y_pick = pick_of(row_ids, n_col * sy)
    place_state(y_state, y_pick, y_init, 0, sy, col, n_col)
    hot_of(row_ids, col * sy, sy, y_column, y_hot, y_init, sy, n_col)
    y_total[...] = jnp.zeros_like(y_total)
    x_total[...] = jnp.zeros_like(x_total)

    last_chunk = CHUNKS - 1

    def gather_of(buffer, now, c, n):
        return buffer[now, c].reshape(n * size, 128)

    def iteration(step, now, first, final):
        z = sliced(z_all, z_send, z_recv, now)
        p = sliced(p_all, p_send, p_recv, now)
        summed = None
        for c in range(CHUNKS):
            col_arrive(*z, c)
            if c > 0:
                col_complete(*z, c - 1)
                term = split_dot(y_hot[c - 1], gather_of(z_all, now, c - 1, n_col))
                summed = term if summed is None else summed + term
        col_complete(*z, last_chunk)

        def new_y(rows, applied):
            old = y_state[rows, :]
            if first:
                return jnp.maximum(old - dual_step * applied, 0.0)
            return jnp.maximum(old + dual_step * (b_state[rows, :] - applied), 0.0)

        z_last = gather_of(z_all, now, last_chunk, n_col)
        mine = slice(0, slots)
        shared = slice(slots, slots + sy)
        y_state[mine, :] = new_y(mine, summed[mine] + split_dot(y_hot[last_chunk, mine, :], z_last))
        if first:
            col_send(*bi, 0)
        products(plain, y_state, lambda c: p_all.at[now, c, row], lambda c: row_send(*p, c))
        y_new = new_y(shared, summed[shared] + split_dot(y_hot[last_chunk, shared, :], z_last))
        y_state[shared, :] = y_new
        if final:
            dual_last[...] = y_new
            dual_mean[...] = (y_total[...] + y_new) / ITERS
        else:
            y_total[...] += y_new
        for c in range(CHUNKS):
            col_sent(*z, c)
        if first:
            row_sent(*xi, 0)
            col_sent(*yi, 0)
            row_arrive(*ci, 0)
            row_sent(*ci, 0)
            place_state(c_state, x_pick, c_init, 0, sx, row, n_row)
            place_state(l_state, x_pick, c_init, sx, sx, row, n_row)
            place_state(u_state, x_pick, c_init, 2 * sx, sx, row, n_row)

        def new_x(rows, transposed):
            moved = x_state[rows, :] - primal_step * (c_state[rows, :] - transposed)
            return jnp.minimum(jnp.maximum(moved, l_state[rows, :]), u_state[rows, :])

        mine = slice(0, slots)
        shared = slice(slots, slots + sx)
        needed = slice(slots if final else 0, slots + sx)
        summed = None
        for c in range(CHUNKS):
            row_arrive(*p, c)
            if c < last_chunk:
                term = split_dot(x_hot[c, needed, :], gather_of(p_all, now, c, n_row))
                summed = term if summed is None else summed + term
        p_last = gather_of(p_all, now, last_chunk, n_row)
        if not final:
            x_old = x_state[mine, :]
            x_new = new_x(mine, summed[mine] + split_dot(x_hot[last_chunk, mine, :], p_last))
            x_state[mine, :] = x_new
            extrapolated[...] = 2.0 * x_new - x_old
            forward(1 - now)
            summed = summed[shared]
        x_new = new_x(shared, summed + split_dot(x_hot[last_chunk, shared, :], p_last))
        if final:
            primal_last[...] = x_new
            primal_mean[...] = (x_total[...] + x_new) / ITERS
        else:
            x_state[shared, :] = x_new
            x_total[...] += x_new
        for c in range(CHUNKS):
            row_sent(*p, c)
        if first:
            col_arrive(*bi, 0)
            col_complete(*bi, 0)
            place_state(b_state, y_pick, b_init, 0, sy, col, n_col)
            col_sent(*bi, 0)

    iteration(0, 0, True, False)

    def middle(step, carry):
        iteration(step, step % 2, False, False)
        return carry

    lax.fori_loop(1, ITERS - 1, middle, 0)
    iteration(ITERS - 1, (ITERS - 1) % 2, False, True)


def in_hbm(array):
    return pltpu.with_memory_space_constraint(array, pltpu.HBM)


def finish(*refs):
    sems = refs[-1]
    copies = [
        pltpu.make_async_copy(source, place, sems.at[i])
        for i, (source, place) in enumerate(zip(refs[:4], refs[4:8]))
    ]
    for copy in copies:
        copy.start()
    for copy in copies:
        copy.wait()


def body(n_row, n_col, tiles, tile_row, tile_col, tile_count, cost, rhs, lower, upper, primal_start, dual_start):
    slots, bs = tiles.shape[0], tiles.shape[2]
    blocks = [a.reshape(-1, bs) for a in (cost, rhs, lower, upper, primal_start, dual_start)]
    sx, sy = blocks[0].shape[0], blocks[1].shape[0]
    f32 = jnp.float32
    chips = n_col // 2
    size = slots // CHUNKS
    vmem = pl.BlockSpec(memory_space=pltpu.VMEM)
    hbm = pl.BlockSpec(memory_space=pltpu.HBM)
    dma = pltpu.SemaphoreType.DMA
    state = lambda share: pltpu.VMEM((slots + share, bs), f32)
    shapes = [jax.ShapeDtypeStruct((s, bs), f32) for s in (sx, sy, sx, sy)]
    out = pl.pallas_call(
        functools.partial(kernel, n_row, n_col),
        out_shape=shapes,
        in_specs=[hbm] * 10,
        out_specs=[vmem] * 4,
        scratch_shapes=[
            pltpu.VMEM(tiles.shape, f32),
            pltpu.VMEM((slots // 2, 2 * bs, 2 * bs), jnp.bfloat16),
            pltpu.VMEM((slots // 2, 2 * bs, 2 * bs), jnp.bfloat16),
            pltpu.VMEM((n_col, sy + SUB, bs), f32),
            pltpu.VMEM((n_row, sx + SUB, bs), f32),
            pltpu.VMEM((n_col, sy, bs), f32),
            pltpu.VMEM((n_row, 3 * sx, bs), f32),
            pltpu.VMEM((2, CHUNKS, n_col, size, bs), f32),
            pltpu.VMEM((2, CHUNKS, n_row, size, bs), f32),
            pltpu.VMEM((CHUNKS, slots + sy, n_col * size), jnp.bfloat16),
            pltpu.VMEM((CHUNKS, slots + sx, n_row * size), jnp.bfloat16),
            pltpu.VMEM((n_col * slots, bs), f32),
            pltpu.VMEM((n_row * slots, bs), f32),
            state(sy), state(sy), state(sx), state(sx), state(sx), state(sx),
            pltpu.VMEM((slots, bs), f32),
            pltpu.VMEM((sy, bs), f32),
            pltpu.VMEM((sx, bs), f32),
            pltpu.VMEM((1, slots), jnp.int32), pltpu.VMEM((1, slots), jnp.int32), pltpu.VMEM((1, 1), jnp.int32),
            dma((TILE_PARTS,)), dma((9,)),
            dma((2, 2 * chips, CHUNKS)), dma((2, 2 * chips, CHUNKS)),
            dma((2, n_row, CHUNKS)), dma((2, n_row, CHUNKS)),
            dma((2 * chips,)), dma((2 * chips,)),
            dma((2 * chips,)), dma((2 * chips,)),
            dma((n_row,)), dma((n_row,)),
            dma((n_row,)), dma((n_row,)),
        ],
        compiler_params=pltpu.CompilerParams(
            collective_id=0, has_side_effects=True, vmem_limit_bytes=VMEM_BYTES
        ),
        name="pdhg",
    )(tiles, in_hbm(tile_row.reshape(1, slots)), in_hbm(tile_col.reshape(1, slots)), tile_count, *map(in_hbm, blocks))
    out = pl.pallas_call(
        finish,
        out_shape=shapes,
        in_specs=[vmem] * 4,
        out_specs=[hbm] * 4,
        scratch_shapes=[dma((4,))],
        compiler_params=pltpu.CompilerParams(vmem_limit_bytes=1024 * 1024),
        name="finish",
    )(*out)
    return tuple(a.reshape(1, -1) for a in out)


def solution(mesh):
    return jax.shard_map(
        functools.partial(body, mesh.shape["row"], mesh.shape["col"]),
        mesh=mesh,
        in_specs=(
            P("row", "col", None),
            P("row", "col"),
            P("row", "col"),
            P("row", "col"),
            P("col", "row"),
            P("row", "col"),
            P("col", "row"),
            P("col", "row"),
            P("col", "row"),
            P("row", "col"),
        ),
        out_specs=(P("col", "row"), P("row", "col"), P("col", "row"), P("row", "col")),
        check_vma=False,
    )
```

```python
import functools

import jax
import jax.numpy as jnp
from jax import lax
from jax.experimental import pallas as pl
from jax.experimental.pallas import tpu as pltpu
from jax.sharding import PartitionSpec as P

ITERS = 6
primal_step = 0.3
dual_step = 0.3
SUB = 8
SHARES = (1, 2, 3)
CHUNKS = len(SHARES)
TILE_PARTS = 4
VMEM_BYTES = 48 * 1024 * 1024


def split_dot(hot, data):
    high = data.astype(jnp.bfloat16)
    rest = data - high.astype(jnp.float32)
    middle = rest.astype(jnp.bfloat16)
    low = (rest - middle.astype(jnp.float32)).astype(jnp.bfloat16)
    dot = functools.partial(jnp.dot, preferred_element_type=jnp.float32)
    return (dot(hot, low) + dot(hot, middle)) + dot(hot, high)


def sum_dot(hot, data):
    high = data.astype(jnp.bfloat16)
    rest = (data - high.astype(jnp.float32)).astype(jnp.bfloat16)
    dot = functools.partial(jnp.dot, preferred_element_type=jnp.float32)
    return dot(hot, rest) + dot(hot, high)


def edges_of(slots):
    return [slots * k // sum(SHARES) // SUB * SUB for k in (sum(SHARES[:i]) for i in range(CHUNKS + 1))]


def pieces_of(data):
    high = data.astype(jnp.bfloat16).astype(jnp.float32)
    rest = data - high
    return high, rest


def kernel(
    n_row, n_col,
    tiles_hbm, tile_row, tile_col, tile_count, cost, rhs, lower, upper, primal_start, dual_start,
    primal_mean, dual_mean, primal_last, dual_last,
    tiles, plain, flipped, y_init, x_init, b_init, c_init, z_all, p_all, y_hot, x_hot, y_column, x_column,
    y_state, b_state, x_state, c_state, l_state, u_state, extrapolated, y_total, x_total,
    row_line, col_line, count_cell, tile_sem, in_sem, z_send, z_recv, p_send, p_recv,
    yi_send, yi_recv, bi_send, bi_recv, xi_send, xi_recv, ci_send, ci_recv,
):
    slots = tile_row.shape[1]
    edges = edges_of(slots)
    sy = rhs.shape[0]
    sx = cost.shape[0]
    row = lax.axis_index("row")
    col = lax.axis_index("col")
    chips = n_col // 2
    chip = col // 2
    core = col % 2
    partner = chip * 2 + (1 - core)
    high_half = (chip * 2) // chips

    def chip_at(k):
        down = chips - 1 - k
        down = down - (chip - down + chips) // chips
        up = k + (k - chip + chips) // chips
        return (1 - high_half) * down + high_half * up

    def row_to(d):
        if n_row == 4:
            return (n_row - 1 - row, (row + 2) % n_row, row + 1 - 2 * (row % 2))[d - 1]
        return (row + d) % n_row

    def row_from(d):
        if n_row == 4:
            return row_to(d)
        return (row + n_row - d) % n_row

    local = [
        pltpu.make_async_copy(source, place, in_sem.at[i])
        for i, (source, place) in enumerate(
            [
                (primal_start, x_init.at[row, 0:sx]),
                (dual_start, y_init.at[col, 0:sy]),
                (rhs, b_init.at[col]),
                (cost, c_init.at[row, 0:sx]),
                (lower, c_init.at[row, sx : 2 * sx]),
                (upper, c_init.at[row, 2 * sx : 3 * sx]),
                (tile_row, row_line),
                (tile_col, col_line),
                (tile_count, count_cell),
            ]
        )
    ]
    for copy in local:
        copy.start()
    part = slots // TILE_PARTS
    tile_copies = [
        pltpu.make_async_copy(
            tiles_hbm.at[i * part : (i + 1) * part], tiles.at[i * part : (i + 1) * part], tile_sem.at[i]
        )
        for i in range(TILE_PARTS)
    ]
    for copy in tile_copies:
        copy.start()

    mesh_id = pl.DeviceIdType.MESH
    barrier = pltpu.get_barrier_semaphore()
    for d in range(1, n_row):
        pl.semaphore_signal(barrier, inc=1, device_id={"row": row_to(d)}, device_id_type=mesh_id)
    for k in range(chips - 1):
        pl.semaphore_signal(
            barrier, inc=1, device_id={"col": chip_at(k) * 2 + core}, device_id_type=mesh_id
        )
    pl.semaphore_signal(barrier, inc=1, device_id={"col": partner}, device_id_type=mesh_id)

    for copy in local[6:]:
        copy.wait()
    live = lax.broadcasted_iota(jnp.int32, (1, slots), 1) < count_cell[...]
    for ids, init, me, at in ((row_line, y_init, col, sy), (col_line, x_init, row, sx)):
        init[me, at : at + SUB, :] = jnp.full((SUB, 128), -1.0, jnp.float32)
        init[me, at : at + SUB, 0:slots] = jnp.broadcast_to(
            jnp.where(live, ids[...].astype(jnp.float32), -1.0), (SUB, slots)
        )

    def remote(place, send, recv, target):
        return pltpu.make_async_remote_copy(
            src_ref=place, dst_ref=place, send_sem=send, recv_sem=recv, device_id=target, device_id_type=mesh_id
        )

    def row_send(place_of, send, recv, c):
        for d in range(1, n_row):
            remote(place_of(row, c), send(d - 1, c), recv(d - 1, c), {"row": row_to(d)}).start()

    def row_arrive(place_of, send, recv, c):
        for d in range(1, n_row):
            remote(place_of(row_from(d), c), send(d - 1, c), recv(d - 1, c), {"row": row_to(d)}).wait_recv()

    def row_sent(place_of, send, recv, c):
        for d in range(1, n_row):
            remote(place_of(row, c), send(d - 1, c), recv(d - 1, c), {"row": row_to(d)}).wait_send()

    to_partner = {"col": partner}

    def col_send(place_of, send, recv, c):
        for k in range(chips - 1):
            there = chip_at(k)
            remote(place_of(col, c), send(there, c), recv(chip, c), {"col": there * 2 + core}).start()
        remote(place_of(col, c), send(chip, c), recv(chip, c), to_partner).start()

    def col_arrive(place_of, send, recv, c):
        for k in reversed(range(chips - 1)):
            there = chip_at(k)
            block = place_of(there * 2 + core, c)
            remote(block, send(there, c), recv(there, c), to_partner).wait_recv()
            remote(block, send(chips + there, c), recv(chips + there, c), to_partner).start()

    def col_complete(place_of, send, recv, c):
        remote(place_of(partner, c), send(chip, c), recv(chip, c), to_partner).wait_recv()
        for k in reversed(range(chips - 1)):
            there = chip_at(k)
            block = place_of(there * 2 + 1 - core, c)
            remote(block, send(chips + there, c), recv(chips + there, c), to_partner).wait_recv()

    def col_sent(place_of, send, recv, c):
        for k in reversed(range(chips - 1)):
            there = chip_at(k)
            remote(place_of(col, c), send(there, c), recv(chip, c), to_partner).wait_send()
            block = place_of(there * 2 + core, c)
            remote(block, send(chips + there, c), recv(chips + there, c), to_partner).wait_send()
        remote(place_of(col, c), send(chip, c), recv(chip, c), to_partner).wait_send()

    def whole(buffer, send, recv):
        return (lambda i, c: buffer.at[i], lambda k, c: send.at[k], lambda k, c: recv.at[k])

    def span(buffer, now, n, i, c):
        size = edges[c + 1] - edges[c]
        return buffer.at[now, pl.ds(pl.multiple_of(n * edges[c] + i * size, SUB), size)]

    def sliced(buffer, send, recv, now, n):
        return (
            lambda i, c: span(buffer, now, n, i, c),
            lambda k, c: send.at[now, k, c],
            lambda k, c: recv.at[now, k, c],
        )

    xi = whole(x_init, xi_send, xi_recv)
    ci = whole(c_init, ci_send, ci_recv)
    yi = whole(y_init, yi_send, yi_recv)
    bi = whole(b_init, bi_send, bi_recv)
    local[0].wait()
    pl.semaphore_wait(barrier, (n_row - 1) + (chips - 1) + 1)
    row_send(*xi, 0)
    for copy in local[1:3]:
        copy.wait()
    y_init[col, 0:sy, :] = y_init[col, 0:sy, :] + dual_step * b_init[col]
    col_send(*yi, 0)

    def pair_up(q, carry):
        for half in range(2):
            tile = tiles[2 * q + half]
            for out, data in ((plain, tile), (flipped, tile.T)):
                high = data.astype(jnp.bfloat16)
                out[q, 0:128, half * 128 : half * 128 + 128] = high
                out[q, 128:256, half * 128 : half * 128 + 128] = (
                    data - high.astype(jnp.float32)
                ).astype(jnp.bfloat16)
        return carry

    for i in range(TILE_PARTS):
        tile_copies[i].wait()
        lax.fori_loop(i * part // 2, (i + 1) * part // 2, pair_up, 0, unroll=2)

    def column_of(init, i, at):
        return init[i, at : at + SUB, :].T[:slots, 0:1]

    def own_ids(init, me, at):
        ids = column_of(init, me, at)
        return jnp.where(ids < 0.0, -2.0, ids)

    def hot_of(ids, first, share, column, hot, init, at, n):
        for i in range(n):
            ids_of = jnp.broadcast_to(column_of(init, i, at), (slots, 128))
            for c in range(CHUNKS):
                size = edges[c + 1] - edges[c]
                start = n * edges[c] + i * size
                column[start : start + size, :] = ids_of[edges[c] : edges[c + 1], :]
        wide_all = column[...].T[0:1, :]
        own = (first + lax.broadcasted_iota(jnp.int32, (share, 1), 0)).astype(jnp.float32)
        for c in range(CHUNKS):
            wide = wide_all[:, n * edges[c] : n * edges[c + 1]]
            width = n * (edges[c + 1] - edges[c])
            hot[c, 0:slots, 0:width] = jnp.where(ids == wide, 1.0, 0.0).astype(jnp.bfloat16)
            hot[c, slots : slots + share, 0:width] = jnp.where(own == wide, 1.0, 0.0).astype(jnp.bfloat16)

    def pick_of(ids, blocks):
        lanes = lax.broadcasted_iota(jnp.int32, (slots, blocks), 1).astype(jnp.float32)
        return jnp.where(ids == lanes, 1.0, 0.0).astype(jnp.bfloat16)

    def place_state(state, pick, init, at, share, me, n):
        state[0:slots, :] = split_dot(pick, init[:, at : at + share, :].reshape(n * share, 128))
        state[slots : slots + share, :] = init[me, at : at + share, :]

    def products(pairs, vectors, out, send):
        line = lax.broadcasted_iota(jnp.int32, (SUB, 128), 0)

        for c in range(CHUNKS):
            place = out(c)

            def group(i, carry):
                g = edges[c] // SUB + i
                at = pl.multiple_of(g * SUB, SUB)
                left = jnp.concatenate(pieces_of(vectors[pl.ds(at, SUB), :]), axis=0).astype(jnp.bfloat16)
                left = jnp.concatenate([left, left], axis=1)
                result = jnp.zeros((SUB, 128), jnp.float32)
                for q in range(SUB // 2):
                    both = jnp.dot(left, pairs[g * (SUB // 2) + q], preferred_element_type=jnp.float32)
                    total = both[SUB:] + both[:SUB]
                    result = jnp.where(line == 2 * q, total[:, :128], result)
                    result = jnp.where(line == 2 * q + 1, total[:, 128:], result)
                place[pl.ds(pl.multiple_of(i * SUB, SUB), SUB), :] = result
                return carry

            lax.fori_loop(0, (edges[c + 1] - edges[c]) // SUB, group, 0, unroll=True)
            send(c)

    def forward(now):
        z = sliced(z_all, z_send, z_recv, now, n_col)
        products(
            flipped, extrapolated, lambda c: span(z_all, now, n_col, col, c), lambda c: col_send(*z, c)
        )

    row_arrive(*xi, 0)
    col_ids = own_ids(x_init, row, sx)
    x_pick = pick_of(col_ids, n_row * sx)
    place_state(x_state, x_pick, x_init, 0, sx, row, n_row)
    extrapolated[...] = x_state[0:slots, :]
    forward(0)
    for copy in local[3:6]:
        copy.wait()
    row_send(*ci, 0)
    hot_of(col_ids, row * sx, sx, x_column, x_hot, x_init, sx, n_row)
    col_arrive(*yi, 0)
    col_complete(*yi, 0)
    row_ids = own_ids(y_init, col, sy)
    y_pick = pick_of(row_ids, n_col * sy)
    place_state(y_state, y_pick, y_init, 0, sy, col, n_col)
    hot_of(row_ids, col * sy, sy, y_column, y_hot, y_init, sy, n_col)
    y_total[...] = jnp.zeros_like(y_total)
    x_total[...] = jnp.zeros_like(x_total)

    last_chunk = CHUNKS - 1

    def gather_of(buffer, now, c, n):
        return buffer[now, n * edges[c] : n * edges[c + 1], :]

    def hot_at(hot, c, rows, n):
        return hot[c, rows, 0 : n * (edges[c + 1] - edges[c])]

    def iteration(step, now, first, final):
        z = sliced(z_all, z_send, z_recv, now, n_col)
        p = sliced(p_all, p_send, p_recv, now, n_row)
        summed = None
        for c in range(CHUNKS):
            col_arrive(*z, c)
            if c > 0:
                col_complete(*z, c - 1)
                term = sum_dot(hot_at(y_hot, c - 1, slice(None), n_col), gather_of(z_all, now, c - 1, n_col))
                summed = term if summed is None else summed + term
        col_complete(*z, last_chunk)

        def new_y(rows, applied):
            old = y_state[rows, :]
            if first:
                return jnp.maximum(old - dual_step * applied, 0.0)
            return jnp.maximum(old + dual_step * (b_state[rows, :] - applied), 0.0)

        z_last = gather_of(z_all, now, last_chunk, n_col)
        mine = slice(0, slots)
        shared = slice(slots, slots + sy)
        y_state[mine, :] = new_y(mine, summed[mine] + sum_dot(hot_at(y_hot, last_chunk, mine, n_col), z_last))
        if first:
            col_send(*bi, 0)
        products(plain, y_state, lambda c: span(p_all, now, n_row, row, c), lambda c: row_send(*p, c))
        y_new = new_y(shared, summed[shared] + sum_dot(hot_at(y_hot, last_chunk, shared, n_col), z_last))
        y_state[shared, :] = y_new
        if final:
            dual_last[...] = y_new
            dual_mean[...] = (y_total[...] + y_new) / ITERS
        else:
            y_total[...] += y_new
        for c in range(CHUNKS):
            col_sent(*z, c)
        if first:
            row_sent(*xi, 0)
            col_sent(*yi, 0)
            row_arrive(*ci, 0)
            row_sent(*ci, 0)
            place_state(c_state, x_pick, c_init, 0, sx, row, n_row)
            place_state(l_state, x_pick, c_init, sx, sx, row, n_row)
            place_state(u_state, x_pick, c_init, 2 * sx, sx, row, n_row)

        def new_x(rows, transposed):
            moved = x_state[rows, :] - primal_step * (c_state[rows, :] - transposed)
            return jnp.minimum(jnp.maximum(moved, l_state[rows, :]), u_state[rows, :])

        mine = slice(0, slots)
        shared = slice(slots, slots + sx)
        needed = slice(slots if final else 0, slots + sx)
        summed = None
        for c in range(CHUNKS):
            row_arrive(*p, c)
            if c < last_chunk:
                term = sum_dot(hot_at(x_hot, c, needed, n_row), gather_of(p_all, now, c, n_row))
                summed = term if summed is None else summed + term
        p_last = gather_of(p_all, now, last_chunk, n_row)
        if not final:
            x_old = x_state[mine, :]
            x_new = new_x(mine, summed[mine] + sum_dot(hot_at(x_hot, last_chunk, mine, n_row), p_last))
            x_state[mine, :] = x_new
            extrapolated[...] = 2.0 * x_new - x_old
            forward(1 - now)
            summed = summed[shared]
        x_new = new_x(shared, summed + sum_dot(hot_at(x_hot, last_chunk, shared, n_row), p_last))
        if final:
            primal_last[...] = x_new
            primal_mean[...] = (x_total[...] + x_new) / ITERS
        else:
            x_state[shared, :] = x_new
            x_total[...] += x_new
        for c in range(CHUNKS):
            row_sent(*p, c)
        if first:
            col_arrive(*bi, 0)
            col_complete(*bi, 0)
            place_state(b_state, y_pick, b_init, 0, sy, col, n_col)
            col_sent(*bi, 0)

    iteration(0, 0, True, False)

    def middle(step, carry):
        iteration(step, step % 2, False, False)
        return carry

    lax.fori_loop(1, ITERS - 1, middle, 0)
    iteration(ITERS - 1, (ITERS - 1) % 2, False, True)


def in_hbm(array):
    return pltpu.with_memory_space_constraint(array, pltpu.HBM)


def finish(*refs):
    sems = refs[-1]
    copies = [
        pltpu.make_async_copy(source, place, sems.at[i])
        for i, (source, place) in enumerate(zip(refs[:4], refs[4:8]))
    ]
    for copy in copies:
        copy.start()
    for copy in copies:
        copy.wait()


def body(n_row, n_col, tiles, tile_row, tile_col, tile_count, cost, rhs, lower, upper, primal_start, dual_start):
    slots, bs = tiles.shape[0], tiles.shape[2]
    blocks = [a.reshape(-1, bs) for a in (cost, rhs, lower, upper, primal_start, dual_start)]
    sx, sy = blocks[0].shape[0], blocks[1].shape[0]
    f32 = jnp.float32
    chips = n_col // 2
    edges = edges_of(slots)
    largest = max(b - a for a, b in zip(edges, edges[1:]))
    vmem = pl.BlockSpec(memory_space=pltpu.VMEM)
    hbm = pl.BlockSpec(memory_space=pltpu.HBM)
    dma = pltpu.SemaphoreType.DMA
    state = lambda share: pltpu.VMEM((slots + share, bs), f32)
    shapes = [jax.ShapeDtypeStruct((s, bs), f32) for s in (sx, sy, sx, sy)]
    out = pl.pallas_call(
        functools.partial(kernel, n_row, n_col),
        out_shape=shapes,
        in_specs=[hbm] * 10,
        out_specs=[vmem] * 4,
        scratch_shapes=[
            pltpu.VMEM(tiles.shape, f32),
            pltpu.VMEM((slots // 2, 2 * bs, 2 * bs), jnp.bfloat16),
            pltpu.VMEM((slots // 2, 2 * bs, 2 * bs), jnp.bfloat16),
            pltpu.VMEM((n_col, sy + SUB, bs), f32),
            pltpu.VMEM((n_row, sx + SUB, bs), f32),
            pltpu.VMEM((n_col, sy, bs), f32),
            pltpu.VMEM((n_row, 3 * sx, bs), f32),
            pltpu.VMEM((2, n_col * slots, bs), f32),
            pltpu.VMEM((2, n_row * slots, bs), f32),
            pltpu.VMEM((CHUNKS, slots + sy, n_col * largest), jnp.bfloat16),
            pltpu.VMEM((CHUNKS, slots + sx, n_row * largest), jnp.bfloat16),
            pltpu.VMEM((n_col * slots, bs), f32),
            pltpu.VMEM((n_row * slots, bs), f32),
            state(sy), state(sy), state(sx), state(sx), state(sx), state(sx),
            pltpu.VMEM((slots, bs), f32),
            pltpu.VMEM((sy, bs), f32),
            pltpu.VMEM((sx, bs), f32),
            pltpu.VMEM((1, slots), jnp.int32), pltpu.VMEM((1, slots), jnp.int32), pltpu.VMEM((1, 1), jnp.int32),
            dma((TILE_PARTS,)), dma((9,)),
            dma((2, 2 * chips, CHUNKS)), dma((2, 2 * chips, CHUNKS)),
            dma((2, n_row, CHUNKS)), dma((2, n_row, CHUNKS)),
            dma((2 * chips,)), dma((2 * chips,)),
            dma((2 * chips,)), dma((2 * chips,)),
            dma((n_row,)), dma((n_row,)),
            dma((n_row,)), dma((n_row,)),
        ],
        compiler_params=pltpu.CompilerParams(
            collective_id=0, has_side_effects=True, vmem_limit_bytes=VMEM_BYTES
        ),
        name="pdhg",
    )(tiles, in_hbm(tile_row.reshape(1, slots)), in_hbm(tile_col.reshape(1, slots)), tile_count, *map(in_hbm, blocks))
    out = pl.pallas_call(
        finish,
        out_shape=shapes,
        in_specs=[vmem] * 4,
        out_specs=[hbm] * 4,
        scratch_shapes=[dma((4,))],
        compiler_params=pltpu.CompilerParams(vmem_limit_bytes=1024 * 1024),
        name="finish",
    )(*out)
    return tuple(a.reshape(1, -1) for a in out)


def solution(mesh):
    return jax.shard_map(
        functools.partial(body, mesh.shape["row"], mesh.shape["col"]),
        mesh=mesh,
        in_specs=(
            P("row", "col", None),
            P("row", "col"),
            P("row", "col"),
            P("row", "col"),
            P("col", "row"),
            P("row", "col"),
            P("col", "row"),
            P("col", "row"),
            P("col", "row"),
            P("row", "col"),
        ),
        out_specs=(P("col", "row"), P("row", "col"), P("col", "row"), P("row", "col")),
        check_vma=False,
    )
```
